32 devices in a mesh: seg: 4 (over y, x), sec: 8 (over z, core).
Axes of the slice: x: 2, y: 2, z: 4, core: 2. Of those that a mesh axis runs over, the one named last changes fastest.
Arguments:
- left_env: bfloat16 [4, 8, 13, 512, 512], P('seg', 'sec'), may hold values from -0.25 to 0.25
- right_env: bfloat16 [4, 8, 13, 512, 512], P('seg', 'sec'), may hold values from -0.25 to 0.25
- left_block: bfloat16 [4, 8, 512, 512], P('seg', 'sec'), may hold values from -8 to 8
- right_block: bfloat16 [4, 8, 512, 512], P('seg', 'sec'), may hold values from -0.25 to 0.25
- inv_sv: bfloat16 [4, 8, 512], P('seg', 'sec'), may hold values from 0.5 to 2
- precond: float32 [4, 8, 512, 512], P('seg', 'sec'), may hold values from 1 to 4
- sector_dims: int32 [4, 8, 2], P('seg', 'sec'), may hold values from 128 to 512, as said below
- channel_charge: int32 [13], replicated, may hold values from -1 to 1
Outputs:
- next_vector: bfloat16 [4, 8, 512, 512], P('seg', 'sec')
- last_image: float32 [4, 8, 512, 512], P('seg', 'sec')
- projected: float32 [4, 4, 4], P('seg')
The draws below stay inside these ranges and needn't reach their ends.
Inputs may be any that keep to these rules, and one draw needn't show every extreme that they name: `sector_dims`: in every segment some sector has left bond dimension 512 and some sector has right bond dimension 512.
All inputs are finite; a program needn't handle non-finite values.
Results may differ from the reference program's by a relative error of at most 0.024.
Values may be sent and summed in bfloat16 or wider, within the bound.
A program may use at most 64 MiB of HBM per device.

```python
import math
import jax
import jax.numpy as jnp
from jax import lax

M = 512
W = 13
MATVECS = 4
SEGS = 4
SECTORS = 8


def draw_sector_dims(key, part):
    first_key, second_key = jax.random.split(jax.random.fold_in(key, 7))
    dims = jax.random.randint(first_key, (SEGS, SECTORS, 2), M // 4, M + 1)
    picked = jax.random.randint(second_key, (SEGS, 2), 0, SECTORS)
    hit = jnp.arange(SECTORS)[None, :, None] == picked[:, None, :]
    return jnp.where(hit, M, dims).astype(jnp.int32)


def draw_left_block(key, part):
    inner_key = jax.random.fold_in(key, 11)
    position = jnp.arange(SECTORS, dtype=jnp.float32) / max(SECTORS - 1, 1)
    factor = jnp.exp(jnp.log(0.4) + position * jnp.log(5.0))
    values = jax.random.normal(inner_key, (SEGS, SECTORS, M, M), jnp.float32)
    return jnp.clip(values * factor[None, :, None, None], -8.0, 8.0).astype(jnp.bfloat16)


def plant(drawn, stream_key, low, high):
    longest = drawn.shape.index(max(drawn.shape))
    spots = []
    for shift in (0, 1):
        where = [jax.random.randint(jax.random.fold_in(stream_key, axis), (), 0, length) for axis, length in enumerate(drawn.shape)]
        where[longest] = (where[longest] + shift) % drawn.shape[longest]
        spots.append(tuple(where))
    return drawn.at[spots[0]].set(low).at[spots[1]].set(high)


def steps_of(stream_key, shape, cuts, low, largest):
    def one(axis_at, shards_of):
        steps = jax.random.uniform(jax.random.fold_in(jax.random.fold_in(stream_key, 6), axis_at), (shards_of,), jnp.float32, low / len(cuts), largest / len(cuts))
        return jnp.repeat(jnp.exp(steps), shape[axis_at] // shards_of).reshape((-1,) + (1,) * (len(shape) - axis_at - 1))

    gain = one(*cuts[0])
    for cut in cuts[1:]:
        gain = gain * one(*cut)
    return gain


def gaussian(stream_key, shape, width, bound, cuts=(), kind=jnp.bfloat16):
    values = width * jax.random.normal(stream_key, shape, jnp.float32)
    if cuts:
        values = values * steps_of(stream_key, shape, cuts, -0.22, 0.18)
    return jnp.clip(values, -bound, bound).astype(kind)


def setup_inputs(seed: int = 0) -> dict:
    splits = jax.random.split(jax.random.key(seed), 9)
    return {
        "left_env": gaussian(splits[0], (SEGS, SECTORS, W, M, M), M ** -0.5, 0.25, ((0, 4), (1, 8))),
        "right_env": gaussian(splits[1], (SEGS, SECTORS, W, M, M), M ** -0.5, 0.25, ((0, 4), (1, 8))),
        "left_block": draw_left_block(jax.random.fold_in(splits[8], 71), 0),
        "right_block": gaussian(splits[3], (SEGS, SECTORS, M, M), M ** -0.5, 0.25, ((0, 4), (1, 8))),
        "inv_sv": jnp.clip(jnp.exp(math.log(2.0) - 1.3862944 * jax.random.uniform(splits[4], (SEGS, SECTORS, M), jnp.float32) ** steps_of(splits[4], (SEGS, SECTORS, M), ((0, 4), (1, 8)), -0.2, 0.2)), 0.5, 2.0).astype(jnp.bfloat16),
        "precond": jnp.clip(jnp.exp(math.log(4.0) - 1.3862944 * jax.random.uniform(splits[5], (SEGS, SECTORS, M, M), jnp.float32) ** steps_of(splits[5], (SEGS, SECTORS, M, M), ((0, 4), (1, 8)), -0.2, 0.2)), 1.0, 4.0),
        "sector_dims": draw_sector_dims(jax.random.fold_in(splits[8], 71), 0),
        "channel_charge": plant(jax.random.randint(splits[7], (W,), -1, 2), jax.random.fold_in(splits[7], 1), -1, 1).astype(jnp.int32),
    }


def reference(left_env, right_env, left_block, right_block, inv_sv, precond, sector_dims, channel_charge):
    eps = 1e-06
    index = jnp.arange(M, dtype=jnp.int32)
    mask = ((index[None, None, :, None] < sector_dims[:, :, 0, None, None]) & (index[None, None, None, :] < sector_dims[:, :, 1, None, None])).astype(jnp.float32)
    count = SECTORS * M * M

    def inner(first, second):
        return lax.optimization_barrier(jnp.sum(first * second, axis=(1, 2, 3))) / count

    def expand(value):
        return value[:, None, None, None]
    neighbour_block = jnp.roll(right_block, -1, axis=0)
    neighbour_inv = jnp.roll(inv_sv, -1, axis=0)
    scaled = (left_block.astype(jnp.float32) * neighbour_inv.astype(jnp.float32)[:, :, None, :]).astype(jnp.bfloat16)
    guess = jnp.einsum('gsab,gsbc->gsac', scaled.astype(jnp.float32), neighbour_block.astype(jnp.float32)) * mask
    first = (guess * expand(lax.rsqrt(inner(guess, guess) + eps))).astype(jnp.bfloat16)
    select = (channel_charge[:, None] == jnp.array([-1, 0, 1], dtype=jnp.int32)[None, :]).astype(jnp.float32)
    left_flat = left_env.reshape(SEGS * SECTORS, W, M, M)
    right_flat = right_env.reshape(SEGS * SECTORS, W, M, M)

    def apply(vector):
        vector_flat = vector.reshape(SEGS * SECTORS, M, M)

        def single(pieces):
            left_one, right_one, vec_one = pieces
            left_x = jnp.einsum('wab,bc->wac', left_one.astype(jnp.float32), vec_one.astype(jnp.float32)).astype(jnp.bfloat16)
            terms = jnp.einsum('wac,wdc->wad', left_x.astype(jnp.float32), right_one.astype(jnp.float32))
            return jnp.stack([lax.optimization_barrier(jnp.sum(terms * select[:, q, None, None], axis=0)) for q in range(3)])
        grouped = lax.map(single, (left_flat, right_flat, vector_flat)).reshape(SEGS, SECTORS, 3, M, M)
        to_lower = grouped[:, :, 0]
        stay = grouped[:, :, 1]
        to_upper = grouped[:, :, 2]
        zero = jnp.zeros_like(stay[:, :1])
        from_lower = jnp.concatenate([zero, to_upper[:, :-1]], axis=1)
        from_upper = jnp.concatenate([to_lower[:, 1:], zero], axis=1)
        return (stay + from_lower + from_upper) * mask
    basis = [first]
    columns = []
    image = None
    for step in range(MATVECS):
        current = basis[step]
        image = apply(current)
        column = [inner(basis[j].astype(jnp.float32), image) for j in range(step + 1)]
        column = column + [jnp.zeros((SEGS,), jnp.float32) for j in range(MATVECS - step - 1)]
        columns.append(jnp.stack(column, axis=1))
        theta = column[step]
        resid = image - expand(theta) * current.astype(jnp.float32)
        correction = resid / precond
        projected_part = jnp.zeros_like(correction)
        for j in range(step + 1):
            weight = inner(basis[j].astype(jnp.float32), correction)
            projected_part = projected_part + expand(weight) * basis[j].astype(jnp.float32)
        remain = correction - projected_part
        basis.append((remain * expand(lax.rsqrt(inner(remain, remain) + eps))).astype(jnp.bfloat16))
    projected = jnp.stack(columns, axis=2)
    return (basis[-1], image, projected)
```

```python
import functools

import jax
import jax.numpy as jnp
from jax import lax
from jax.experimental import pallas as pl
from jax.experimental.pallas import tpu as pltpu
from jax.sharding import PartitionSpec as P

MATVECS = 4
EPS = 1e-06
ROWS = 128
CHUNK = 32
MESH = pl.DeviceIdType.MESH


def fold(values):
    rows, columns = values.shape
    block = jnp.sum(values.reshape(rows // 8, 8, columns), axis=0)
    total = block[:, :128]
    for at in range(128, columns, 128):
        total = total + block[:, at : at + 128]
    return total


def kernel(
    segs, secs,
    charge_ref, dims_ref, left_hbm, right_hbm, block_ref, other_hbm, inv_ref, precond_ref,
    next_ref, image_ref, projected_ref,
    left_ref, right_ref, nb_ref, ninv_ref, scaled_ref, pinv_ref, basis_ref, lx_ref, prefix_ref,
    stay_ref, up_out, low_out, up_in, low_in, slots_ref, rows_ref, gram_ref, proj_ref, order_ref,
    load_sem, guess_send, guess_recv, halo_send, halo_recv, sum_send, sum_recv,
):
    channels, width, _ = left_ref.shape
    tiles = width // ROWS
    count = secs * width * width
    f32, bf16 = jnp.float32, jnp.bfloat16
    seg, sec = lax.axis_index("seg"), lax.axis_index("sec")
    seg_before = lax.rem(seg + segs - 1, segs)
    seg_after = lax.rem(seg + 1, segs)

    load_left = pltpu.make_async_copy(left_hbm, left_ref, load_sem.at[0])
    load_right = pltpu.make_async_copy(right_hbm, right_ref, load_sem.at[1])
    load_left.start()
    load_right.start()

    barrier = pltpu.get_barrier_semaphore()
    pl.semaphore_signal(barrier, inc=1, device_id=(seg_before, sec), device_id_type=MESH)
    pl.semaphore_signal(barrier, inc=1, device_id=(seg_after, sec), device_id_type=MESH)
    for offset in range(1, secs):
        peer = lax.rem(sec + offset, secs)
        pl.semaphore_signal(barrier, inc=1, device_id=(seg, peer), device_id_type=MESH)
    pl.semaphore_wait(barrier, secs + 1)

    def remote(src, dst, send, recv, device):
        return pltpu.make_async_remote_copy(
            src_ref=src, dst_ref=dst, send_sem=send, recv_sem=recv,
            device_id=device, device_id_type=MESH,
        )

    send_inv = remote(
        inv_ref, ninv_ref, guess_send.at[0], guess_recv.at[0], (seg_before, sec)
    )
    send_block = remote(
        other_hbm, nb_ref, guess_send.at[1], guess_recv.at[1], (seg_before, sec)
    )
    send_inv.start()
    send_block.start()

    keys = []
    for w in range(channels):
        q = charge_ref[w]
        keys.append(jnp.where(q == 1, 0, jnp.where(q == -1, 1, 2)))
    raising = jnp.int32(0)
    moving = jnp.int32(0)
    for w in range(channels):
        raising = raising + jnp.where(keys[w] == 0, 1, 0)
        moving = moving + jnp.where(keys[w] <= 1, 1, 0)
    places = []
    for w in range(channels):
        place = jnp.int32(0)
        for v in range(channels):
            if v < w:
                place = place + jnp.where(keys[v] <= keys[w], 1, 0)
            elif v > w:
                place = place + jnp.where(keys[v] < keys[w], 1, 0)
        places.append(place)
    for i in range(channels):
        who = jnp.int32(0)
        for w in range(channels):
            who = who + jnp.where(places[w] == i, w, 0)
        order_ref[i] = who

    gram_ref[...] = jnp.zeros_like(gram_ref)
    rows_ref[...] = jnp.zeros_like(rows_ref)
    proj_ref[...] = jnp.zeros_like(proj_ref)

    @pl.loop(0, width // CHUNK)
    def _(c):
        at = pl.ds(pl.multiple_of(c * CHUNK, CHUNK), CHUNK)
        pinv_ref[at, :] = 1.0 / precond_ref[at, :]
        for k in range(1, MATVECS):
            basis_ref[k, at, :] = jnp.zeros((CHUNK, width), bf16)

    @pl.loop(0, ROWS // CHUNK)
    def _(c):
        at = pl.ds(pl.multiple_of(c * CHUNK, CHUNK), CHUNK)
        prefix_ref[0, at, :] = jnp.zeros((CHUNK, width), f32)

    @pl.when(sec == 0)
    def _():
        @pl.loop(0, MATVECS * tiles)
        def _(n):
            up_in[n] = jnp.zeros((ROWS, width), bf16)

    @pl.when(sec == secs - 1)
    def _():
        @pl.loop(0, MATVECS * tiles)
        def _(n):
            low_in[n] = jnp.zeros((ROWS, width), bf16)

    def masked(values, start):
        row = start + lax.broadcasted_iota(jnp.int32, values.shape, 0)
        column = lax.broadcasted_iota(jnp.int32, values.shape, 1)
        inside = (row < dims_ref[0]) & (column < dims_ref[1])
        return jnp.where(inside, values, 0.0)

    def sum_copies(r):
        own = slots_ref.at[r, sec]
        return [
            remote(
                own, own, sum_send.at[r], sum_recv.at[r],
                (seg, lax.rem(sec + offset, secs)),
            )
            for offset in range(1, secs)
        ]

    def total(r, tile):
        slots_ref[r, sec] = tile
        for copy in sum_copies(r):
            copy.start()
        arrived = slots_ref.at[r, pl.ds(0, secs - 1)]
        pltpu.make_async_copy(arrived, arrived, sum_recv.at[r]).wait()
        return jnp.sum(slots_ref[r], axis=0) * (1.0 / count)

    send_inv.wait_recv()
    scaled_ref[...] = (
        block_ref[...].astype(f32) * ninv_ref[...].astype(f32)
    ).astype(bf16)
    send_block.wait_recv()

    @pl.loop(0, tiles)
    def _(t):
        at = pl.ds(pl.multiple_of(t * ROWS, ROWS), ROWS)
        image_ref[at, :] = masked(
            jnp.dot(scaled_ref[at, :], nb_ref[...], preferred_element_type=f32), t * ROWS
        )

    def square(c, carry):
        part = image_ref[pl.ds(pl.multiple_of(c * CHUNK, CHUNK), CHUNK), :]
        return carry + fold(part * part)

    guess_sq = lax.fori_loop(0, width // CHUNK, square, jnp.zeros((8, 128), f32))
    guess_sq = jnp.sum(total(0, guess_sq), axis=(0, 1), keepdims=True)
    scale = lax.rsqrt(guess_sq + EPS)

    @pl.loop(0, width // CHUNK)
    def _(c):
        at = pl.ds(pl.multiple_of(c * CHUNK, CHUNK), CHUNK)
        basis_ref[0, at, :] = (image_ref[at, :] * scale).astype(bf16)

    load_left.wait()
    load_right.wait()

    def up_copy(n):
        return remote(
            up_out.at[n], up_in.at[n], halo_send.at[0, n], halo_recv.at[0, n],
            (seg, lax.rem(sec + 1, secs)),
        )

    def low_copy(n):
        return remote(
            low_out.at[n], low_in.at[n], halo_send.at[1, n], halo_recv.at[1, n],
            (seg, lax.rem(sec + secs - 1, secs)),
        )

    @pl.loop(0, MATVECS)
    def _(k):
        def process(t, carry):
            n = k * tiles + t

            @pl.when(sec > 0)
            def _():
                up_copy(n).wait_recv()

            @pl.when(sec < secs - 1)
            def _():
                low_copy(n).wait_recv()

            def body(c, carry):
                inner = pl.ds(pl.multiple_of(c * CHUNK, CHUNK), CHUNK)
                start = t * ROWS + c * CHUNK
                at = pl.ds(pl.multiple_of(start, CHUNK), CHUNK)
                image = stay_ref[at, :] + up_in[n, inner, :].astype(f32)
                image = masked(image + low_in[n, inner, :].astype(f32), start)
                image_ref[at, :] = image
                pinv = pinv_ref[at, :]
                lifted = image * pinv
                new = []
                for j in range(MATVECS):
                    vector = basis_ref[j, at, :].astype(f32)
                    new.append(fold(vector * image))
                    new.append(fold(vector * lifted))
                new.append(fold(lifted * lifted))
                lifted_x = basis_ref[k, at, :].astype(f32) * pinv
                new.append(fold(lifted * lifted_x))
                return tuple(a + b for a, b in zip(carry, new))

            return lax.fori_loop(0, ROWS // CHUNK, body, carry)

        def step(t, carry):
            n = k * tiles + t
            at = pl.ds(pl.multiple_of(t * ROWS, ROWS), ROWS)
            vector = basis_ref[k]
            for w in range(channels):
                lx_ref[w] = jnp.dot(
                    left_ref[w, at, :], vector, preferred_element_type=f32
                ).astype(bf16)
            for i in range(channels):
                w = order_ref[i]
                term = lax.dot_general(
                    lx_ref[w], right_ref[w], (((1,), (1,)), ((), ())),
                    preferred_element_type=f32,
                )
                prefix_ref[i + 1] = prefix_ref[i] + term
            first = prefix_ref[raising]
            second = prefix_ref[moving]
            up_out[n] = first.astype(bf16)
            low_out[n] = (second - first).astype(bf16)

            @pl.when(sec < secs - 1)
            def _():
                up_copy(n).start()

            @pl.when(sec > 0)
            def _():
                low_copy(n).start()

            stay_ref[at, :] = prefix_ref[channels] - second
            return carry

        zeros = tuple(jnp.zeros((8, 128), f32) for _ in range(2 * MATVECS + 2))
        step(0, 0)

        def pipelined(t, carry):
            step(t, 0)
            return process(t - 1, carry)

        carry = lax.fori_loop(1, tiles, pipelined, zeros)

        def own(c, carry):
            at = pl.ds(pl.multiple_of(c * CHUNK, CHUNK), CHUNK)
            current = basis_ref[k, at, :].astype(f32)
            lifted = current * pinv_ref[at, :]
            new = []
            for j in range(MATVECS):
                vector = basis_ref[j, at, :].astype(f32)
                new.append(fold(vector * current))
                new.append(fold(vector * lifted))
            new.append(fold(lifted * lifted))
            return tuple(a + b for a, b in zip(carry, new))

        own_carry = lax.fori_loop(
            0, width // CHUNK, own,
            tuple(jnp.zeros((8, 128), f32) for _ in range(2 * MATVECS + 1)),
        )
        carry = process(tiles - 1, carry)

        def put(row, value):
            rows_ref[row : row + 1, :] = jnp.sum(value, axis=0, keepdims=True)

        for j in range(MATVECS):
            put(j, carry[2 * j])
            put(4 + j, own_carry[2 * j])
            put(8 + j, carry[2 * j + 1])
            put(12 + j, own_carry[2 * j + 1])
        put(16, carry[2 * MATVECS])
        put(17, carry[2 * MATVECS + 1])
        put(18, own_carry[2 * MATVECS])
        sums = jnp.sum(rows_ref[...], axis=1, keepdims=True)
        lane = lax.broadcasted_iota(jnp.int32, (8, 128), 1)
        tile = jnp.where(
            lane == 0, sums[0:8], jnp.where(lane == 1, sums[8:16], sums[16:24])
        )
        tile = total(k + 1, tile)
        gram_ref[k] = tile
        proj_ref[...] = jnp.where(lane == k, tile[:, 0:1], proj_ref[...])

        def entry(source, row, at):
            return source[row : row + 1, at : at + 1]

        row = lax.broadcasted_iota(jnp.int32, (8, 128), 0)
        theta = jnp.sum(
            jnp.where((row == k) & (lane == 0), tile, 0.0), axis=(0, 1), keepdims=True
        )
        weights = [
            entry(tile, j, 1) - theta * entry(tile, 4 + j, 1) for j in range(MATVECS)
        ]
        norm_sq = (
            entry(tile, 0, 2) - 2.0 * theta * entry(tile, 1, 2)
            + theta * theta * entry(tile, 2, 2)
        )
        for i in range(MATVECS):
            column = gram_ref[i]
            inner = weights[i] * entry(column, 4 + i, 0) - 2.0 * weights[i]
            for j in range(i):
                inner = inner + 2.0 * weights[j] * entry(column, 4 + j, 0)
            norm_sq = norm_sq + weights[i] * inner
        scale = lax.rsqrt(jnp.maximum(norm_sq, 0.0) + EPS)

        def update(c, target):
            at = pl.ds(pl.multiple_of(c * CHUNK, CHUNK), CHUNK)
            current = basis_ref[k, at, :].astype(f32)
            remain = (image_ref[at, :] - theta * current) * pinv_ref[at, :]
            for j in range(MATVECS):
                remain = remain - weights[j] * basis_ref[j, at, :].astype(f32)
            target[at, :] = (remain * scale).astype(bf16)

        @pl.loop(0, width // CHUNK)
        def _(c):
            update(c, basis_ref.at[k + 1])

    @pl.loop(0, width // CHUNK)
    def _(c):
        at = pl.ds(pl.multiple_of(c * CHUNK, CHUNK), CHUNK)
        next_ref[at, :] = basis_ref[MATVECS, at, :]

    projected_ref[...] = proj_ref[:MATVECS, :MATVECS]

    send_inv.wait_send()
    send_block.wait_send()

    @pl.when(sec < secs - 1)
    def _():
        @pl.loop(0, MATVECS * tiles)
        def _(n):
            up_copy(n).wait_send()

    @pl.when(sec > 0)
    def _():
        @pl.loop(0, MATVECS * tiles)
        def _(n):
            low_copy(n).wait_send()

    @pl.loop(0, MATVECS + 1)
    def _(r):
        sent = slots_ref.at[r, pl.ds(0, secs - 1)]
        pltpu.make_async_copy(sent, sent, sum_send.at[r]).wait()


def per_device(
    left_env, right_env, left_block, right_block, inv_sv, precond, sector_dims, channel_charge
):
    segs, secs = lax.axis_size("seg"), lax.axis_size("sec")
    channels, width = left_env.shape[2], left_env.shape[-1]
    tiles = width // ROWS
    halos = MATVECS * tiles
    f32, bf16 = jnp.float32, jnp.bfloat16
    vmem = pl.BlockSpec(memory_space=pltpu.VMEM)
    smem = pl.BlockSpec(memory_space=pltpu.SMEM)
    hbm = pl.BlockSpec(memory_space=pl.ANY)
    following, image, projected = pl.pallas_call(
        functools.partial(kernel, segs, secs),
        name="davidson",
        out_shape=(
            jax.ShapeDtypeStruct((width, width), bf16),
            jax.ShapeDtypeStruct((width, width), f32),
            jax.ShapeDtypeStruct((MATVECS, MATVECS), f32),
        ),
        in_specs=[smem, smem, hbm, hbm, vmem, hbm, vmem, vmem],
        out_specs=(vmem, vmem, vmem),
        scratch_shapes=[
            pltpu.VMEM((channels, width, width), bf16),
            pltpu.VMEM((channels, width, width), bf16),
            pltpu.VMEM((width, width), bf16),
            pltpu.VMEM((1, width), bf16),
            pltpu.VMEM((width, width), bf16),
            pltpu.VMEM((width, width), f32),
            pltpu.VMEM((MATVECS + 1, width, width), bf16),
            pltpu.VMEM((channels, ROWS, width), bf16),
            pltpu.VMEM((channels + 1, ROWS, width), f32),
            pltpu.VMEM((width, width), f32),
            pltpu.VMEM((halos, ROWS, width), bf16),
            pltpu.VMEM((halos, ROWS, width), bf16),
            pltpu.VMEM((halos, ROWS, width), bf16),
            pltpu.VMEM((halos, ROWS, width), bf16),
            pltpu.VMEM((MATVECS + 1, secs, 8, 128), f32),
            pltpu.VMEM((24, 128), f32),
            pltpu.VMEM((MATVECS, 8, 128), f32),
            pltpu.VMEM((8, 128), f32),
            pltpu.SMEM((channels,), jnp.int32),
            pltpu.SemaphoreType.DMA((2,)),
            pltpu.SemaphoreType.DMA((2,)),
            pltpu.SemaphoreType.DMA((2,)),
            pltpu.SemaphoreType.DMA((2, halos)),
            pltpu.SemaphoreType.DMA((2, halos)),
            pltpu.SemaphoreType.DMA((MATVECS + 1,)),
            pltpu.SemaphoreType.DMA((MATVECS + 1,)),
        ],
        compiler_params=pltpu.CompilerParams(
            collective_id=0, has_side_effects=True, vmem_limit_bytes=60 * 1024 * 1024
        ),
    )(
        channel_charge, sector_dims[0, 0], left_env[0, 0], right_env[0, 0],
        left_block[0, 0], right_block[0, 0], inv_sv[0], precond[0, 0],
    )
    return following[None, None], image[None, None], projected[None]


def solution(mesh):
    in_specs = (
        P("seg", "sec", None, None, None),
        P("seg", "sec", None, None, None),
        P("seg", "sec", None, None),
        P("seg", "sec", None, None),
        P("seg", "sec", None),
        P("seg", "sec", None, None),
        P("seg", "sec", None),
        P(),
    )
    out_specs = (P("seg", "sec", None, None), P("seg", "sec", None, None), P("seg", None, None))
    return jax.shard_map(
        per_device, mesh=mesh, in_specs=in_specs, out_specs=out_specs, check_vma=False
    )
```

```python
import functools

import jax
import jax.numpy as jnp
from jax import lax
from jax.experimental import pallas as pl
from jax.experimental.pallas import tpu as pltpu
from jax.sharding import PartitionSpec as P

MATVECS = 4
EPS = 1e-06
ROWS = 256
COLS = 256
CHUNK = 32
BLOCK = 64
MESH = pl.DeviceIdType.MESH


def fold(values):
    rows, columns = values.shape
    block = jnp.sum(values.reshape(rows // 8, 8, columns), axis=0)
    total = block[:, :128]
    for at in range(128, columns, 128):
        total = total + block[:, at : at + 128]
    return total


def kernel(
    segs, secs,
    charge_ref, dims_ref, left_hbm, right_hbm, block_hbm, other_hbm, inv_ref, precond_hbm,
    next_ref, image_ref, projected_ref,
    left_ref, right_ref, block_ref, precond_ref, nb_ref, ninv_ref, scaled_ref, pinv_ref, basis_ref, lx_ref, prefix_ref,
    stay_ref, up_out, low_out, up_in, low_in, slots_ref, rows_ref, gram_ref, proj_ref, order_ref,
    load_sem, guess_send, guess_recv, halo_send, halo_recv, sum_send, sum_recv,
):
    channels, width, _ = left_ref.shape
    tiles = width // ROWS
    halves = width // COLS
    pieces = tiles * halves
    count = secs * width * width
    f32, bf16 = jnp.float32, jnp.bfloat16
    seg, sec = lax.axis_index("seg"), lax.axis_index("sec")
    seg_before = lax.rem(seg + segs - 1, segs)
    seg_after = lax.rem(seg + 1, segs)

    load_left = pltpu.make_async_copy(left_hbm, left_ref, load_sem.at[0])
    load_right = pltpu.make_async_copy(right_hbm, right_ref, load_sem.at[1])
    load_block = pltpu.make_async_copy(block_hbm, block_ref, load_sem.at[2])
    load_precond = pltpu.make_async_copy(precond_hbm, precond_ref, load_sem.at[3])
    load_precond.start()
    load_block.start()
    load_left.start()
    load_right.start()

    barrier = pltpu.get_barrier_semaphore()
    pl.semaphore_signal(barrier, inc=1, device_id=(seg_before, sec), device_id_type=MESH)
    pl.semaphore_signal(barrier, inc=1, device_id=(seg_after, sec), device_id_type=MESH)
    for offset in range(1, secs):
        peer = lax.rem(sec + offset, secs)
        pl.semaphore_signal(barrier, inc=1, device_id=(seg, peer), device_id_type=MESH)
    pl.semaphore_wait(barrier, secs + 1)

    def remote(src, dst, send, recv, device):
        return pltpu.make_async_remote_copy(
            src_ref=src, dst_ref=dst, send_sem=send, recv_sem=recv,
            device_id=device, device_id_type=MESH,
        )

    send_inv = remote(
        inv_ref, ninv_ref, guess_send.at[0], guess_recv.at[0], (seg_before, sec)
    )
    send_block = remote(
        other_hbm, nb_ref, guess_send.at[1], guess_recv.at[1], (seg_before, sec)
    )
    send_inv.start()
    send_block.start()

    keys = []
    for w in range(channels):
        q = charge_ref[w]
        keys.append(jnp.where(q == 1, 0, jnp.where(q == -1, 1, 2)))
    raising = jnp.int32(0)
    moving = jnp.int32(0)
    for w in range(channels):
        raising = raising + jnp.where(keys[w] == 0, 1, 0)
        moving = moving + jnp.where(keys[w] <= 1, 1, 0)
    places = []
    for w in range(channels):
        place = jnp.int32(0)
        for v in range(channels):
            if v < w:
                place = place + jnp.where(keys[v] <= keys[w], 1, 0)
            elif v > w:
                place = place + jnp.where(keys[v] < keys[w], 1, 0)
        places.append(place)
    for i in range(channels):
        who = jnp.int32(0)
        for w in range(channels):
            who = who + jnp.where(places[w] == i, w, 0)
        order_ref[i] = who

    load_precond.wait()
    gram_ref[...] = jnp.zeros_like(gram_ref)
    rows_ref[...] = jnp.zeros_like(rows_ref)
    proj_ref[...] = jnp.zeros_like(proj_ref)

    @pl.loop(0, width // CHUNK)
    def _(c):
        at = pl.ds(pl.multiple_of(c * CHUNK, CHUNK), CHUNK)
        pinv_ref[at, :] = 1.0 / precond_ref[at, :]
        for k in range(1, MATVECS):
            basis_ref[k, at, :] = jnp.zeros((CHUNK, width), bf16)

    @pl.loop(0, ROWS // CHUNK)
    def _(c):
        at = pl.ds(pl.multiple_of(c * CHUNK, CHUNK), CHUNK)
        prefix_ref[0, at, :] = jnp.zeros((CHUNK, COLS), f32)

    @pl.when(sec == 0)
    def _():
        @pl.loop(0, MATVECS * pieces)
        def _(n):
            up_in[n] = jnp.zeros((ROWS, COLS), bf16)

    @pl.when(sec == secs - 1)
    def _():
        @pl.loop(0, MATVECS * pieces)
        def _(n):
            low_in[n] = jnp.zeros((ROWS, COLS), bf16)

    def masked(values, start, left=0):
        row = start + lax.broadcasted_iota(jnp.int32, values.shape, 0)
        column = left + lax.broadcasted_iota(jnp.int32, values.shape, 1)
        inside = (row < dims_ref[0]) & (column < dims_ref[1])
        return jnp.where(inside, values, 0.0)

    def sum_copies(r):
        own = slots_ref.at[r, sec]
        return [
            remote(
                own, own, sum_send.at[r], sum_recv.at[r],
                (seg, lax.rem(sec + offset, secs)),
            )
            for offset in range(1, secs)
        ]

    def total(r, tile):
        slots_ref[r, sec] = tile
        for copy in sum_copies(r):
            copy.start()
        arrived = slots_ref.at[r, pl.ds(0, secs - 1)]
        pltpu.make_async_copy(arrived, arrived, sum_recv.at[r]).wait()
        return jnp.sum(slots_ref[r], axis=0) * (1.0 / count)

    send_inv.wait_recv()
    load_block.wait()
    scaled_ref[...] = (
        block_ref[...].astype(f32) * ninv_ref[...].astype(f32)
    ).astype(bf16)
    send_block.wait_recv()

    @pl.loop(0, tiles)
    def _(t):
        at = pl.ds(pl.multiple_of(t * ROWS, ROWS), ROWS)
        image_ref[at, :] = masked(
            jnp.dot(scaled_ref[at, :], nb_ref[...], preferred_element_type=f32), t * ROWS
        )

    def square(c, carry):
        part = image_ref[pl.ds(pl.multiple_of(c * CHUNK, CHUNK), CHUNK), :]
        return carry + fold(part * part)

    guess_sq = lax.fori_loop(0, width // CHUNK, square, jnp.zeros((8, 128), f32))
    rows_ref[19:20, :] = jnp.sum(guess_sq, axis=0, keepdims=True)

    @pl.loop(0, width // CHUNK)
    def _(c):
        at = pl.ds(pl.multiple_of(c * CHUNK, CHUNK), CHUNK)
        basis_ref[0, at, :] = image_ref[at, :].astype(bf16)

    load_left.wait()
    load_right.wait()

    def up_copy(n):
        return remote(
            up_out.at[n], up_in.at[n], halo_send.at[0, n], halo_recv.at[0, n],
            (seg, lax.rem(sec + 1, secs)),
        )

    def low_copy(n):
        return remote(
            low_out.at[n], low_in.at[n], halo_send.at[1, n], halo_recv.at[1, n],
            (seg, lax.rem(sec + secs - 1, secs)),
        )

    @pl.loop(0, MATVECS)
    def _(k):
        def process(piece, carry):
            t, h = divmod(piece, halves)
            n = k * pieces + piece
            across = pl.ds(h * COLS, COLS)

            @pl.when(sec > 0)
            def _():
                up_copy(n).wait_recv()

            @pl.when(sec < secs - 1)
            def _():
                low_copy(n).wait_recv()

            def body(c, carry):
                inner = pl.ds(pl.multiple_of(c * BLOCK, BLOCK), BLOCK)
                start = t * ROWS + c * BLOCK
                at = pl.ds(pl.multiple_of(start, BLOCK), BLOCK)
                image = stay_ref[at, across] + up_in[n, inner, :].astype(f32)
                image = masked(image + low_in[n, inner, :].astype(f32), start, h * COLS)
                image_ref[at, across] = image
                pinv = pinv_ref[at, across]
                lifted = image * pinv
                new = []
                for j in range(MATVECS):
                    vector = basis_ref[j, at, across].astype(f32)
                    new.append(fold(vector * image))
                    new.append(fold(vector * lifted))
                new.append(fold(lifted * lifted))
                lifted_x = basis_ref[k, at, across].astype(f32) * pinv
                new.append(fold(lifted * lifted_x))
                return tuple(a + b for a, b in zip(carry, new))

            return lax.fori_loop(0, ROWS // BLOCK, body, carry)

        for t in range(tiles):
            rows = pl.ds(t * ROWS, ROWS)
            vector = basis_ref[k]
            for w in range(channels):
                lx_ref[w] = jnp.dot(
                    left_ref[w, rows, :], vector, preferred_element_type=f32
                ).astype(bf16)
            for h in range(halves):
                n = k * pieces + t * halves + h
                across = pl.ds(h * COLS, COLS)
                for i in range(channels):
                    w = order_ref[i]
                    term = lax.dot_general(
                        lx_ref[w], right_ref[w, across, :], (((1,), (1,)), ((), ())),
                        preferred_element_type=f32,
                    )
                    prefix_ref[i + 1] = prefix_ref[i] + term
                first = prefix_ref[raising]
                second = prefix_ref[moving]
                up_out[n] = first.astype(bf16)
                low_out[n] = (second - first).astype(bf16)

                @pl.when(sec < secs - 1)
                def _():
                    up_copy(n).start()

                @pl.when(sec > 0)
                def _():
                    low_copy(n).start()

                stay_ref[rows, across] = prefix_ref[channels] - second

        def own(c, carry):
            at = pl.ds(pl.multiple_of(c * CHUNK, CHUNK), CHUNK)
            current = basis_ref[k, at, :].astype(f32)
            lifted = current * pinv_ref[at, :]
            new = []
            for j in range(MATVECS):
                vector = basis_ref[j, at, :].astype(f32)
                new.append(fold(vector * current))
                new.append(fold(vector * lifted))
            new.append(fold(lifted * lifted))
            return tuple(a + b for a, b in zip(carry, new))

        own_carry = lax.fori_loop(
            0, width // CHUNK, own,
            tuple(jnp.zeros((8, 128), f32) for _ in range(2 * MATVECS + 1)),
        )
        carry = tuple(jnp.zeros((8, 128), f32) for _ in range(2 * MATVECS + 2))
        for piece in range(pieces):
            carry = process(piece, carry)

        def put(row, value):
            rows_ref[row : row + 1, :] = jnp.sum(value, axis=0, keepdims=True)

        for j in range(MATVECS):
            put(j, carry[2 * j])
            put(4 + j, own_carry[2 * j])
            put(8 + j, carry[2 * j + 1])
            put(12 + j, own_carry[2 * j + 1])
        put(16, carry[2 * MATVECS])
        put(17, carry[2 * MATVECS + 1])
        put(18, own_carry[2 * MATVECS])
        sums = jnp.sum(rows_ref[...], axis=1, keepdims=True)
        lane = lax.broadcasted_iota(jnp.int32, (8, 128), 1)
        tile = jnp.where(
            lane == 0, sums[0:8], jnp.where(lane == 1, sums[8:16], sums[16:24])
        )
        tile = total(k, tile)

        def entry(source, row, at):
            return source[row : row + 1, at : at + 1]

        guess_scale = lax.rsqrt(entry(tile, 3, 2) + EPS)
        factor = jnp.where(k == 0, guess_scale, 1.0)
        tile = tile * (factor * factor)
        gram_ref[k] = tile
        proj_ref[...] = jnp.where(lane == k, tile[:, 0:1], proj_ref[...])

        row = lax.broadcasted_iota(jnp.int32, (8, 128), 0)
        theta = jnp.sum(
            jnp.where((row == k) & (lane == 0), tile, 0.0), axis=(0, 1), keepdims=True
        )
        weights = [
            entry(tile, j, 1) - theta * entry(tile, 4 + j, 1) for j in range(MATVECS)
        ]
        norm_sq = (
            entry(tile, 0, 2) - 2.0 * theta * entry(tile, 1, 2)
            + theta * theta * entry(tile, 2, 2)
        )
        for i in range(MATVECS):
            column = gram_ref[i]
            inner = weights[i] * entry(column, 4 + i, 0) - 2.0 * weights[i]
            for j in range(i):
                inner = inner + 2.0 * weights[j] * entry(column, 4 + j, 0)
            norm_sq = norm_sq + weights[i] * inner
        scale = lax.rsqrt(jnp.maximum(norm_sq, 0.0) + EPS)

        @pl.when(k == 0)
        def _():
            @pl.loop(0, width // CHUNK)
            def _(c):
                at = pl.ds(pl.multiple_of(c * CHUNK, CHUNK), CHUNK)
                basis_ref[0, at, :] = (basis_ref[0, at, :].astype(f32) * guess_scale).astype(bf16)

        def update(c, target):
            at = pl.ds(pl.multiple_of(c * CHUNK, CHUNK), CHUNK)
            current = basis_ref[k, at, :].astype(f32)
            remain = (image_ref[at, :] * factor - theta * current) * pinv_ref[at, :]
            for j in range(MATVECS):
                remain = remain - weights[j] * basis_ref[j, at, :].astype(f32)
            target[at, :] = (remain * scale).astype(bf16)

        @pl.loop(0, width // CHUNK)
        def _(c):
            update(c, basis_ref.at[k + 1])

    @pl.loop(0, width // CHUNK)
    def _(c):
        at = pl.ds(pl.multiple_of(c * CHUNK, CHUNK), CHUNK)
        next_ref[at, :] = basis_ref[MATVECS, at, :]

    projected_ref[...] = proj_ref[:MATVECS, :MATVECS]

    send_inv.wait_send()
    send_block.wait_send()

    @pl.when(sec < secs - 1)
    def _():
        @pl.loop(0, MATVECS * pieces)
        def _(n):
            up_copy(n).wait_send()

    @pl.when(sec > 0)
    def _():
        @pl.loop(0, MATVECS * pieces)
        def _(n):
            low_copy(n).wait_send()

    @pl.loop(0, MATVECS)
    def _(r):
        sent = slots_ref.at[r, pl.ds(0, secs - 1)]
        pltpu.make_async_copy(sent, sent, sum_send.at[r]).wait()


def finish(next_in, image_in, projected_in, next_ref, image_ref, projected_ref):
    next_ref[...] = next_in[...]
    image_ref[...] = image_in[...]
    projected_ref[...] = projected_in[...]


def per_device(
    left_env, right_env, left_block, right_block, inv_sv, precond, sector_dims, channel_charge
):
    segs, secs = lax.axis_size("seg"), lax.axis_size("sec")
    channels, width = left_env.shape[2], left_env.shape[-1]
    halos = MATVECS * (width // ROWS) * (width // COLS)
    f32, bf16 = jnp.float32, jnp.bfloat16
    vmem = pl.BlockSpec(memory_space=pltpu.VMEM)
    smem = pl.BlockSpec(memory_space=pltpu.SMEM)
    hbm = pl.BlockSpec(memory_space=pl.ANY)
    out_shape = (
        jax.ShapeDtypeStruct((width, width), bf16),
        jax.ShapeDtypeStruct((width, width), f32),
        jax.ShapeDtypeStruct((MATVECS, MATVECS), f32),
    )
    results = pl.pallas_call(
        functools.partial(kernel, segs, secs),
        name="davidson",
        out_shape=out_shape,
        in_specs=[smem, smem, hbm, hbm, hbm, hbm, vmem, hbm],
        out_specs=(vmem, vmem, vmem),
        scratch_shapes=[
            pltpu.VMEM((channels, width, width), bf16),
            pltpu.VMEM((channels, width, width), bf16),
            pltpu.VMEM((width, width), bf16),
            pltpu.VMEM((width, width), f32),
            pltpu.VMEM((width, width), bf16),
            pltpu.VMEM((1, width), bf16),
            pltpu.VMEM((width, width), bf16),
            pltpu.VMEM((width, width), f32),
            pltpu.VMEM((MATVECS + 1, width, width), bf16),
            pltpu.VMEM((channels, ROWS, width), bf16),
            pltpu.VMEM((channels + 1, ROWS, COLS), f32),
            pltpu.VMEM((width, width), f32),
            pltpu.VMEM((halos, ROWS, COLS), bf16),
            pltpu.VMEM((halos, ROWS, COLS), bf16),
            pltpu.VMEM((halos, ROWS, COLS), bf16),
            pltpu.VMEM((halos, ROWS, COLS), bf16),
            pltpu.VMEM((MATVECS, secs, 8, 128), f32),
            pltpu.VMEM((24, 128), f32),
            pltpu.VMEM((MATVECS, 8, 128), f32),
            pltpu.VMEM((8, 128), f32),
            pltpu.SMEM((channels,), jnp.int32),
            pltpu.SemaphoreType.DMA((4,)),
            pltpu.SemaphoreType.DMA((2,)),
            pltpu.SemaphoreType.DMA((2,)),
            pltpu.SemaphoreType.DMA((2, halos)),
            pltpu.SemaphoreType.DMA((2, halos)),
            pltpu.SemaphoreType.DMA((MATVECS,)),
            pltpu.SemaphoreType.DMA((MATVECS,)),
        ],
        compiler_params=pltpu.CompilerParams(
            collective_id=0, has_side_effects=True, vmem_limit_bytes=60 * 1024 * 1024
        ),
    )(
        channel_charge, sector_dims[0, 0], left_env[0, 0], right_env[0, 0],
        left_block[0, 0], right_block[0, 0], inv_sv[0], precond[0, 0],
    )
    following, image, projected = pl.pallas_call(
        finish, name="finish", out_shape=out_shape,
        in_specs=[vmem] * 3, out_specs=(vmem, vmem, vmem),
    )(*results)
    return following[None, None], image[None, None], projected[None]


def solution(mesh):
    in_specs = (
        P("seg", "sec", None, None, None),
        P("seg", "sec", None, None, None),
        P("seg", "sec", None, None),
        P("seg", "sec", None, None),
        P("seg", "sec", None),
        P("seg", "sec", None, None),
        P("seg", "sec", None),
        P(),
    )
    out_specs = (P("seg", "sec", None, None), P("seg", "sec", None, None), P("seg", None, None))
    return jax.shard_map(
        per_device, mesh=mesh, in_specs=in_specs, out_specs=out_specs, check_vma=False
    )
```

```python
import functools

import jax
import jax.numpy as jnp
from jax import lax
from jax.experimental import pallas as pl
from jax.experimental.pallas import tpu as pltpu
from jax.sharding import PartitionSpec as P

MATVECS = 4
EPS = 1e-06
ROWS = 256
COLS = 256
CHUNK = 32
BLOCK = 64
MESH = pl.DeviceIdType.MESH


def fold(values):
    rows, columns = values.shape
    block = jnp.sum(values.reshape(rows // 8, 8, columns), axis=0)
    total = block[:, :128]
    for at in range(128, columns, 128):
        total = total + block[:, at : at + 128]
    return total


def kernel(
    segs, secs,
    charge_ref, dims_ref, left_hbm, right_hbm, block_hbm, other_hbm, inv_ref, precond_hbm,
    next_ref, image_ref, projected_ref,
    left_ref, right_ref, block_ref, precond_ref, nb_ref, ninv_ref, scaled_ref, pinv_ref, basis_ref, lx_ref, prefix_ref,
    stay_ref, up_out, low_out, up_in, low_in, slots_ref, rows_ref, gram_ref, proj_ref, order_ref,
    load_sem, guess_send, guess_recv, halo_send, halo_recv, sum_send, sum_recv,
):
    channels, width, _ = left_ref.shape
    tiles = width // ROWS
    halves = width // COLS
    pieces = tiles * halves
    count = secs * width * width
    f32, bf16 = jnp.float32, jnp.bfloat16
    seg, sec = lax.axis_index("seg"), lax.axis_index("sec")
    seg_before = lax.rem(seg + segs - 1, segs)
    seg_after = lax.rem(seg + 1, segs)

    load_left = pltpu.make_async_copy(left_hbm, left_ref, load_sem.at[0])
    load_right = pltpu.make_async_copy(right_hbm, right_ref, load_sem.at[1])
    load_block = pltpu.make_async_copy(block_hbm, block_ref, load_sem.at[2])
    load_precond = pltpu.make_async_copy(precond_hbm, precond_ref, load_sem.at[3])
    load_precond.start()
    load_block.start()
    load_left.start()
    load_right.start()

    barrier = pltpu.get_barrier_semaphore()
    pl.semaphore_signal(barrier, inc=1, device_id=(seg_before, sec), device_id_type=MESH)
    pl.semaphore_signal(barrier, inc=1, device_id=(seg_after, sec), device_id_type=MESH)
    for offset in range(1, secs):
        peer = lax.rem(sec + offset, secs)
        pl.semaphore_signal(barrier, inc=1, device_id=(seg, peer), device_id_type=MESH)
    pl.semaphore_wait(barrier, secs + 1)

    def remote(src, dst, send, recv, device):
        return pltpu.make_async_remote_copy(
            src_ref=src, dst_ref=dst, send_sem=send, recv_sem=recv,
            device_id=device, device_id_type=MESH,
        )

    send_inv = remote(
        inv_ref, ninv_ref, guess_send.at[0], guess_recv.at[0], (seg_before, sec)
    )
    send_block = remote(
        other_hbm, nb_ref, guess_send.at[1], guess_recv.at[1], (seg_before, sec)
    )
    send_inv.start()
    send_block.start()

    keys = []
    for w in range(channels):
        q = charge_ref[w]
        keys.append(jnp.where(q == 1, 0, jnp.where(q == -1, 1, 2)))
    raising = jnp.int32(0)
    moving = jnp.int32(0)
    for w in range(channels):
        raising = raising + jnp.where(keys[w] == 0, 1, 0)
        moving = moving + jnp.where(keys[w] <= 1, 1, 0)
    places = []
    for w in range(channels):
        place = jnp.int32(0)
        for v in range(channels):
            if v < w:
                place = place + jnp.where(keys[v] <= keys[w], 1, 0)
            elif v > w:
                place = place + jnp.where(keys[v] < keys[w], 1, 0)
        places.append(place)
    for i in range(channels):
        who = jnp.int32(0)
        for w in range(channels):
            who = who + jnp.where(places[w] == i, w, 0)
        order_ref[i] = who

    load_precond.wait()
    gram_ref[...] = jnp.zeros_like(gram_ref)
    rows_ref[...] = jnp.zeros_like(rows_ref)
    proj_ref[...] = jnp.zeros_like(proj_ref)

    @pl.loop(0, width // CHUNK)
    def _(c):
        at = pl.ds(pl.multiple_of(c * CHUNK, CHUNK), CHUNK)
        pinv_ref[at, :] = 1.0 / precond_ref[at, :]
        for k in range(1, MATVECS):
            basis_ref[k, at, :] = jnp.zeros((CHUNK, width), bf16)

    @pl.loop(0, ROWS // CHUNK)
    def _(c):
        at = pl.ds(pl.multiple_of(c * CHUNK, CHUNK), CHUNK)
        prefix_ref[0, at, :] = jnp.zeros((CHUNK, COLS), f32)

    @pl.when(sec == 0)
    def _():
        @pl.loop(0, MATVECS * pieces)
        def _(n):
            up_in[n] = jnp.zeros((ROWS, COLS), bf16)

    @pl.when(sec == secs - 1)
    def _():
        @pl.loop(0, MATVECS * pieces)
        def _(n):
            low_in[n] = jnp.zeros((ROWS, COLS), bf16)

    def masked(values, start, left=0):
        row = start + lax.broadcasted_iota(jnp.int32, values.shape, 0)
        column = left + lax.broadcasted_iota(jnp.int32, values.shape, 1)
        inside = (row < dims_ref[0]) & (column < dims_ref[1])
        return jnp.where(inside, values, 0.0)

    def sum_copies(r):
        own = slots_ref.at[r, sec]
        return [
            remote(
                own, own, sum_send.at[r], sum_recv.at[r],
                (seg, lax.rem(sec + offset, secs)),
            )
            for offset in range(1, secs)
        ]

    def total(r, tile):
        slots_ref[r, sec] = tile
        for copy in sum_copies(r):
            copy.start()
        arrived = slots_ref.at[r, pl.ds(0, secs - 1)]
        pltpu.make_async_copy(arrived, arrived, sum_recv.at[r]).wait()
        return jnp.sum(slots_ref[r], axis=0) * (1.0 / count)

    send_inv.wait_recv()
    load_block.wait()
    scaled_ref[...] = (
        block_ref[...].astype(f32) * ninv_ref[...].astype(f32)
    ).astype(bf16)
    send_block.wait_recv()

    @pl.loop(0, tiles)
    def _(t):
        at = pl.ds(pl.multiple_of(t * ROWS, ROWS), ROWS)
        image_ref[at, :] = masked(
            jnp.dot(scaled_ref[at, :], nb_ref[...], preferred_element_type=f32), t * ROWS
        )

    def square(c, carry):
        part = image_ref[pl.ds(pl.multiple_of(c * CHUNK, CHUNK), CHUNK), :]
        return carry + fold(part * part)

    guess_sq = lax.fori_loop(0, width // CHUNK, square, jnp.zeros((8, 128), f32))
    rows_ref[19:20, :] = jnp.sum(guess_sq, axis=0, keepdims=True)

    @pl.loop(0, width // CHUNK)
    def _(c):
        at = pl.ds(pl.multiple_of(c * CHUNK, CHUNK), CHUNK)
        basis_ref[0, at, :] = image_ref[at, :].astype(bf16)

    load_left.wait()
    load_right.wait()

    def up_copy(n):
        return remote(
            up_out.at[n], up_in.at[n], halo_send.at[0, n], halo_recv.at[0, n],
            (seg, lax.rem(sec + 1, secs)),
        )

    def low_copy(n):
        return remote(
            low_out.at[n], low_in.at[n], halo_send.at[1, n], halo_recv.at[1, n],
            (seg, lax.rem(sec + secs - 1, secs)),
        )

    @pl.loop(0, MATVECS)
    def _(k):
        def process(kk, piece, carry):
            t, h = divmod(piece, halves)
            n = k * pieces + piece
            across = pl.ds(h * COLS, COLS)

            @pl.when(sec > 0)
            def _():
                up_copy(n).wait_recv()

            @pl.when(sec < secs - 1)
            def _():
                low_copy(n).wait_recv()

            def body(c, carry):
                inner = pl.ds(pl.multiple_of(c * BLOCK, BLOCK), BLOCK)
                start = t * ROWS + c * BLOCK
                at = pl.ds(pl.multiple_of(start, BLOCK), BLOCK)
                image = stay_ref[at, across] + up_in[n, inner, :].astype(f32)
                image = masked(image + low_in[n, inner, :].astype(f32), start, h * COLS)
                image_ref[at, across] = image
                pinv = pinv_ref[at, across]
                lifted = image * pinv
                new = []
                for j in range(kk + 1):
                    vector = basis_ref[j, at, across].astype(f32)
                    new.append(fold(vector * image))
                    new.append(fold(vector * lifted))
                new.append(fold(lifted * lifted))
                lifted_x = basis_ref[k, at, across].astype(f32) * pinv
                new.append(fold(lifted * lifted_x))
                return tuple(a + b for a, b in zip(carry, new))

            return lax.fori_loop(0, ROWS // BLOCK, body, carry)

        for t in range(tiles):
            rows = pl.ds(t * ROWS, ROWS)
            vector = basis_ref[k]
            for w in range(channels):
                lx_ref[w] = jnp.dot(
                    left_ref[w, rows, :], vector, preferred_element_type=f32
                ).astype(bf16)
            for h in range(halves):
                n = k * pieces + t * halves + h
                across = pl.ds(h * COLS, COLS)
                for i in range(channels):
                    w = order_ref[i]
                    term = lax.dot_general(
                        lx_ref[w], right_ref[w, across, :], (((1,), (1,)), ((), ())),
                        preferred_element_type=f32,
                    )
                    prefix_ref[i + 1] = prefix_ref[i] + term
                first = prefix_ref[raising]
                second = prefix_ref[moving]
                up_out[n] = first.astype(bf16)
                low_out[n] = (second - first).astype(bf16)

                @pl.when(sec < secs - 1)
                def _():
                    up_copy(n).start()

                @pl.when(sec > 0)
                def _():
                    low_copy(n).start()

                stay_ref[rows, across] = prefix_ref[channels] - second

        def put(row, value):
            rows_ref[row : row + 1, :] = jnp.sum(value, axis=0, keepdims=True)

        def reduce(kk):
            def own(c, carry):
                at = pl.ds(pl.multiple_of(c * CHUNK, CHUNK), CHUNK)
                current = basis_ref[kk, at, :].astype(f32)
                lifted = current * pinv_ref[at, :]
                new = []
                for j in range(kk + 1):
                    vector = basis_ref[j, at, :].astype(f32)
                    new.append(fold(vector * current))
                    new.append(fold(vector * lifted))
                new.append(fold(lifted * lifted))
                return tuple(a + b for a, b in zip(carry, new))

            zero = jnp.zeros((8, 128), f32)
            own_carry = lax.fori_loop(0, width // CHUNK, own, (zero,) * (2 * kk + 3))
            carry = (zero,) * (2 * kk + 4)
            for piece in range(pieces):
                carry = process(kk, piece, carry)
            for j in range(kk + 1):
                put(j, carry[2 * j])
                put(4 + j, own_carry[2 * j])
                put(8 + j, carry[2 * j + 1])
                put(12 + j, own_carry[2 * j + 1])
            put(16, carry[2 * kk + 2])
            put(17, carry[2 * kk + 3])
            put(18, own_carry[2 * kk + 2])

        for kk in range(MATVECS):
            pl.when(k == kk)(functools.partial(reduce, kk))

        sums = jnp.sum(rows_ref[...], axis=1, keepdims=True)
        lane = lax.broadcasted_iota(jnp.int32, (8, 128), 1)
        tile = jnp.where(
            lane == 0, sums[0:8], jnp.where(lane == 1, sums[8:16], sums[16:24])
        )
        tile = total(k, tile)

        def entry(source, row, at):
            return source[row : row + 1, at : at + 1]

        guess_scale = lax.rsqrt(entry(tile, 3, 2) + EPS)
        factor = jnp.where(k == 0, guess_scale, 1.0)
        tile = tile * (factor * factor)
        gram_ref[k] = tile
        proj_ref[...] = jnp.where(lane == k, tile[:, 0:1], proj_ref[...])

        row = lax.broadcasted_iota(jnp.int32, (8, 128), 0)
        theta = jnp.sum(
            jnp.where((row == k) & (lane == 0), tile, 0.0), axis=(0, 1), keepdims=True
        )
        weights = [
            entry(tile, j, 1) - theta * entry(tile, 4 + j, 1) for j in range(MATVECS)
        ]
        norm_sq = (
            entry(tile, 0, 2) - 2.0 * theta * entry(tile, 1, 2)
            + theta * theta * entry(tile, 2, 2)
        )
        for i in range(MATVECS):
            column = gram_ref[i]
            inner = weights[i] * entry(column, 4 + i, 0) - 2.0 * weights[i]
            for j in range(i):
                inner = inner + 2.0 * weights[j] * entry(column, 4 + j, 0)
            norm_sq = norm_sq + weights[i] * inner
        scale = lax.rsqrt(jnp.maximum(norm_sq, 0.0) + EPS)

        @pl.when(k == 0)
        def _():
            @pl.loop(0, width // CHUNK)
            def _(c):
                at = pl.ds(pl.multiple_of(c * CHUNK, CHUNK), CHUNK)
                basis_ref[0, at, :] = (basis_ref[0, at, :].astype(f32) * guess_scale).astype(bf16)

        def update(kk):
            @pl.loop(0, width // CHUNK)
            def _(c):
                at = pl.ds(pl.multiple_of(c * CHUNK, CHUNK), CHUNK)
                image = image_ref[at, :]
                if kk == 0:
                    image = image * factor
                current = basis_ref[kk, at, :].astype(f32)
                remain = (image - theta * current) * pinv_ref[at, :]
                for j in range(kk + 1):
                    remain = remain - weights[j] * basis_ref[j, at, :].astype(f32)
                basis_ref[kk + 1, at, :] = (remain * scale).astype(bf16)

        for kk in range(MATVECS):
            pl.when(k == kk)(functools.partial(update, kk))

    @pl.loop(0, width // CHUNK)
    def _(c):
        at = pl.ds(pl.multiple_of(c * CHUNK, CHUNK), CHUNK)
        next_ref[at, :] = basis_ref[MATVECS, at, :]

    projected_ref[...] = proj_ref[:MATVECS, :MATVECS]

    send_inv.wait_send()
    send_block.wait_send()

    @pl.when(sec < secs - 1)
    def _():
        @pl.loop(0, MATVECS * pieces)
        def _(n):
            up_copy(n).wait_send()

    @pl.when(sec > 0)
    def _():
        @pl.loop(0, MATVECS * pieces)
        def _(n):
            low_copy(n).wait_send()

    @pl.loop(0, MATVECS)
    def _(r):
        sent = slots_ref.at[r, pl.ds(0, secs - 1)]
        pltpu.make_async_copy(sent, sent, sum_send.at[r]).wait()


def finish(next_in, image_in, projected_in, next_ref, image_ref, projected_ref):
    next_ref[...] = next_in[...]
    image_ref[...] = image_in[...]
    projected_ref[...] = projected_in[...]


def per_device(
    left_env, right_env, left_block, right_block, inv_sv, precond, sector_dims, channel_charge
):
    segs, secs = lax.axis_size("seg"), lax.axis_size("sec")
    channels, width = left_env.shape[2], left_env.shape[-1]
    halos = MATVECS * (width // ROWS) * (width // COLS)
    f32, bf16 = jnp.float32, jnp.bfloat16
    vmem = pl.BlockSpec(memory_space=pltpu.VMEM)
    smem = pl.BlockSpec(memory_space=pltpu.SMEM)
    hbm = pl.BlockSpec(memory_space=pl.ANY)
    out_shape = (
        jax.ShapeDtypeStruct((width, width), bf16),
        jax.ShapeDtypeStruct((width, width), f32),
        jax.ShapeDtypeStruct((MATVECS, MATVECS), f32),
    )
    results = pl.pallas_call(
        functools.partial(kernel, segs, secs),
        name="davidson",
        out_shape=out_shape,
        in_specs=[smem, smem, hbm, hbm, hbm, hbm, vmem, hbm],
        out_specs=(vmem, vmem, vmem),
        scratch_shapes=[
            pltpu.VMEM((channels, width, width), bf16),
            pltpu.VMEM((channels, width, width), bf16),
            pltpu.VMEM((width, width), bf16),
            pltpu.VMEM((width, width), f32),
            pltpu.VMEM((width, width), bf16),
            pltpu.VMEM((1, width), bf16),
            pltpu.VMEM((width, width), bf16),
            pltpu.VMEM((width, width), f32),
            pltpu.VMEM((MATVECS + 1, width, width), bf16),
            pltpu.VMEM((channels, ROWS, width), bf16),
            pltpu.VMEM((channels + 1, ROWS, COLS), f32),
            pltpu.VMEM((width, width), f32),
            pltpu.VMEM((halos, ROWS, COLS), bf16),
            pltpu.VMEM((halos, ROWS, COLS), bf16),
            pltpu.VMEM((halos, ROWS, COLS), bf16),
            pltpu.VMEM((halos, ROWS, COLS), bf16),
            pltpu.VMEM((MATVECS, secs, 8, 128), f32),
            pltpu.VMEM((24, 128), f32),
            pltpu.VMEM((MATVECS, 8, 128), f32),
            pltpu.VMEM((8, 128), f32),
            pltpu.SMEM((channels,), jnp.int32),
            pltpu.SemaphoreType.DMA((4,)),
            pltpu.SemaphoreType.DMA((2,)),
            pltpu.SemaphoreType.DMA((2,)),
            pltpu.SemaphoreType.DMA((2, halos)),
            pltpu.SemaphoreType.DMA((2, halos)),
            pltpu.SemaphoreType.DMA((MATVECS,)),
            pltpu.SemaphoreType.DMA((MATVECS,)),
        ],
        compiler_params=pltpu.CompilerParams(
            collective_id=0, has_side_effects=True, vmem_limit_bytes=60 * 1024 * 1024
        ),
    )(
        channel_charge, sector_dims[0, 0], left_env[0, 0], right_env[0, 0],
        left_block[0, 0], right_block[0, 0], inv_sv[0], precond[0, 0],
    )
    following, image, projected = pl.pallas_call(
        finish, name="finish", out_shape=out_shape,
        in_specs=[vmem] * 3, out_specs=(vmem, vmem, vmem),
    )(*results)
    return following[None, None], image[None, None], projected[None]


def solution(mesh):
    in_specs = (
        P("seg", "sec", None, None, None),
        P("seg", "sec", None, None, None),
        P("seg", "sec", None, None),
        P("seg", "sec", None, None),
        P("seg", "sec", None),
        P("seg", "sec", None, None),
        P("seg", "sec", None),
        P(),
    )
    out_specs = (P("seg", "sec", None, None), P("seg", "sec", None, None), P("seg", None, None))
    return jax.shard_map(
        per_device, mesh=mesh, in_specs=in_specs, out_specs=out_specs, check_vma=False
    )
```
